32 devices in a mesh: head: 4 (over y, x), tok: 8 (over z, core).
Axes of the slice: x: 2, y: 2, z: 4, core: 2. Of those that a mesh axis runs over, the one named last changes fastest.
Arguments:
- queries: bfloat16 [2, 2048, 5120], P(None, 'tok', 'head'), may hold values from -6 to 6
- key_rows: bfloat16 [2048, 5120], P('tok', 'head'), may hold values from -6 to 6
- value_rows: bfloat16 [2048, 5120], P('tok', 'head'), may hold values from -6 to 6
- step_rates: float32 [20, 2048], P('head', 'tok'), may hold values from 0.05 to 1
- gate_fast: float32 [20, 256, 256], P('head'), may hold values from -0.375 to 0.375
- up_fast: float32 [20, 256, 256], P('head'), may hold values from -0.375 to 0.375
- down_fast: float32 [20, 256, 256], P('head'), may hold values from -0.375 to 0.375
Outputs:
- out_rows: bfloat16 [2, 2048, 5120], P(None, ('tok', 'head'))
The draws below stay inside these ranges and needn't reach their ends.
All inputs are finite; a program needn't handle non-finite values.
Results may differ from the reference program's by a relative error of at most 0.011.
Values may be sent and summed in bfloat16 or wider, within the bound.
A program may use at most 64 MiB of HBM per device.

```python
import math
import jax
import jax.numpy as jnp
from jax import lax

HD = 256
FH = 256
NS_STEPS = 3
HEADS = 20
BLOCK = 2048


def level_of(own_key, dims, cuts, smallest, largest):
    def one(axis_at, shards_of):
        draws = jax.random.uniform(jax.random.fold_in(jax.random.fold_in(own_key, 6), axis_at), (shards_of,), jnp.float32, smallest / len(cuts), largest / len(cuts))
        return jnp.repeat(jnp.exp(draws), dims[axis_at] // shards_of).reshape((-1,) + (1,) * (len(dims) - axis_at - 1))

    gain = one(*cuts[0])
    for cut in cuts[1:]:
        gain = gain * one(*cut)
    return gain


def noise(own_key, dims, deviation, most, shards=(), dtype=jnp.bfloat16):
    loudness = level_of(own_key, dims, shards, -0.22, 0.18) if shards else 1.0
    array = jax.random.normal(own_key, dims, jnp.float32) * deviation * loudness
    return jnp.minimum(jnp.maximum(array, -most), most).astype(dtype)


def setup_inputs(seed: int = 0) -> dict:
    seeds = jax.random.split(jax.random.key(seed), 8)
    queries = noise(seeds[0], (2, BLOCK, HEADS * HD), 1.0, 6.0, ((1, 8), (2, 4)))
    key_rows = noise(seeds[1], (BLOCK, HEADS * HD), 1.0, 6.0, ((0, 8), (1, 4)))
    value_rows = noise(seeds[2], (BLOCK, HEADS * HD), 1.0, 6.0, ((0, 8), (1, 4)))
    step_rates = jnp.clip(jnp.exp(math.log(1.0) - 2.9957323 * jax.random.uniform(seeds[3], (HEADS, BLOCK), jnp.float32) ** level_of(seeds[3], (HEADS, BLOCK), ((0, 4), (1, 8)), -0.2, 0.2)), 0.05, 1.0)
    gate_fast = noise(seeds[4], (HEADS, HD, FH), HD ** -0.5, 0.375, ((0, 4),), jnp.float32)
    up_fast = noise(seeds[5], (HEADS, HD, FH), HD ** -0.5, 0.375, ((0, 4),), jnp.float32)
    down_fast = noise(seeds[6], (HEADS, FH, HD), FH ** -0.5, 0.375, ((0, 4),), jnp.float32)
    return dict(queries=queries, key_rows=key_rows, value_rows=value_rows, step_rates=step_rates, gate_fast=gate_fast, up_fast=up_fast, down_fast=down_fast)


coef_first = 3.4445
coef_second = -4.775
coef_third = 2.0315

def fast_apply(inputs, gate_mat, up_mat, down_mat):
    gate_pre = jnp.dot(inputs, gate_mat, preferred_element_type=jnp.float32)
    up_pre = jnp.dot(inputs, up_mat, preferred_element_type=jnp.float32)
    hidden = (jax.nn.silu(gate_pre) * up_pre).astype(jnp.bfloat16)
    return jnp.dot(hidden, down_mat, preferred_element_type=jnp.float32).astype(jnp.bfloat16)

def orthogonal(gradient):
    iterate = gradient / (jnp.sqrt(jnp.sum(gradient * gradient)) + 1e-07)
    for sweep in range(NS_STEPS):
        gram = jnp.dot(iterate.T, iterate, precision=lax.Precision.HIGHEST)
        square = jnp.dot(gram, gram, precision=lax.Precision.HIGHEST)
        poly = coef_second * gram + coef_third * square
        iterate = coef_first * iterate + jnp.dot(iterate, poly, precision=lax.Precision.HIGHEST)
    return iterate

def head_layer(pieces):
    first_query, second_query, key_head, value_head, rates, gate_fast, up_fast, down_fast = pieces
    gate_half = gate_fast.astype(jnp.bfloat16)
    up_half = up_fast.astype(jnp.bfloat16)
    down_half = down_fast.astype(jnp.bfloat16)
    first = fast_apply(first_query, gate_half, up_half, down_half)
    gate_pre = jnp.dot(key_head, gate_half, preferred_element_type=jnp.float32)
    up_pre = jnp.dot(key_head, up_half, preferred_element_type=jnp.float32)
    sigmoid_gate = jax.nn.sigmoid(gate_pre)
    hidden = (jax.nn.silu(gate_pre) * up_pre).astype(jnp.bfloat16)
    down_in = (-(rates[:, None] * value_head.astype(jnp.float32))).astype(jnp.bfloat16)
    down_grad = jnp.dot(hidden.T, down_in, preferred_element_type=jnp.float32)
    hidden_grad = jnp.dot(down_in, down_half.T, preferred_element_type=jnp.float32)
    up_in = (hidden_grad * jax.nn.silu(gate_pre)).astype(jnp.bfloat16)
    gate_in = (hidden_grad * up_pre * sigmoid_gate * (1.0 + gate_pre * (1.0 - sigmoid_gate))).astype(jnp.bfloat16)
    gate_grad = jnp.dot(key_head.T, gate_in, preferred_element_type=jnp.float32)
    up_grad = jnp.dot(key_head.T, up_in, preferred_element_type=jnp.float32)
    gate_next = (gate_fast - orthogonal(gate_grad)).astype(jnp.bfloat16)
    up_next = (up_fast - orthogonal(up_grad)).astype(jnp.bfloat16)
    down_next = (down_fast - orthogonal(down_grad)).astype(jnp.bfloat16)
    second = fast_apply(second_query, gate_next, up_next, down_next)
    return (first, second)

def reference(queries, key_rows, value_rows, step_rates, gate_fast, up_fast, down_fast):
    query_heads = queries.reshape(2, BLOCK, HEADS, HD).transpose(2, 0, 1, 3)
    key_heads = key_rows.reshape(BLOCK, HEADS, HD).transpose(1, 0, 2)
    value_heads = value_rows.reshape(BLOCK, HEADS, HD).transpose(1, 0, 2)
    first, second = lax.map(head_layer, (query_heads[:, 0], query_heads[:, 1], key_heads, value_heads, step_rates, gate_fast, up_fast, down_fast))
    joined = jnp.stack((first, second), 0)
    return joined.transpose(0, 2, 1, 3).reshape(2, BLOCK, HEADS * HD)
```

```python
import functools

import jax
import jax.numpy as jnp
from jax import lax
from jax.experimental import pallas as pl
from jax.experimental.pallas import tpu as pltpu
from jax.sharding import PartitionSpec as P

NS_STEPS = 3
KINDS = 3
PIECES = 2
LAG = 2

coef_first = 3.4445
coef_second = -4.775
coef_third = 2.0315

MESH = pl.DeviceIdType.MESH
BF = jnp.bfloat16
F32 = jnp.float32


def mm(a, b):
    return jnp.dot(a, b, preferred_element_type=F32)


def mm_tn(a, b):
    return lax.dot_general(a, b, (((0,), (0,)), ((), ())), preferred_element_type=F32)


def mm_nt(a, b):
    return lax.dot_general(a, b, (((1,), (1,)), ((), ())), preferred_element_type=F32)


def fast_apply(x, gate, up, down):
    pre = mm(x, gate)
    hidden = (pre / (1.0 + jnp.exp(-pre)) * mm(x, up)).astype(BF)
    return mm(hidden, down).astype(BF)


def kernel(
    nh, nz, q_in, k_in, v_in, rates, g_in, u_in, d_in, out,
    qb, kb, vb, wf, wh, gb, pb, cs, cr, wn, ob,
    in_sem, ps_s, ps_r, ch_s, ch_r, ag_s, ag_r, ap_s, ap_r, a_s, a_r, a_l,
):
    heads, rows, size = kb.shape
    count = KINDS * heads
    pairs = pb.shape[0]
    piece = size // PIECES
    share = rows // nh
    hd = lax.axis_index("head")
    tok = lax.axis_index("tok")
    lane = lax.rem(tok, 2)
    z = tok // 2
    partner = (hd, z * 2 + 1 - lane)

    def cut(h):
        return pl.ds(h * size if isinstance(h, int) else pl.multiple_of(h * size, size), size)

    def load(at, h):
        src, dst = (
            (k_in.at[:, cut(h)], kb.at[h]),
            (g_in.at[h], wf.at[0, h]),
            (u_in.at[h], wf.at[1, h]),
            (v_in.at[:, cut(h)], vb.at[h]),
            (d_in.at[h], wf.at[2, h]),
            (q_in.at[0, :, cut(h)], qb.at[0, h]),
            (q_in.at[1, :, cut(h)], qb.at[1, h]),
        )[at]
        return pltpu.make_async_copy(src, dst, in_sem.at[at, h])

    for h in range(heads):
        for at in range(5):
            load(at, h).start()
    for h in range(heads):
        for at in (5, 6):
            load(at, h).start()

    barrier = pltpu.get_barrier_semaphore()
    pl.semaphore_signal(barrier, inc=1, device_id=partner, device_id_type=MESH)
    for p in range(1, nh):
        pl.semaphore_signal(
            barrier, inc=1, device_id=(lax.rem(hd + p, nh), tok), device_id_type=MESH
        )

    @pl.when(z > 0)
    def _():
        pl.semaphore_signal(barrier, inc=1, device_id=(hd, tok - 2), device_id_type=MESH)

    @pl.when(z < nz - 1)
    def _():
        pl.semaphore_signal(barrier, inc=1, device_id=(hd, tok + 2), device_id_type=MESH)

    inner = (z > 0).astype(jnp.int32) + (z < nz - 1).astype(jnp.int32)
    pl.semaphore_wait(barrier, nh + inner)

    def mine(j):
        return 2 * j + lane

    def side(j):
        return lax.rem(j, 2)

    def is_start(j):
        return z == (1 - side(j)) * (nz - 1)

    def is_owner(j):
        return z == side(j) * (nz - 1)

    def towards(j):
        return (hd, tok + (2 * side(j) - 1) * 2)

    def back(j):
        return (hd, tok - (2 * side(j) - 1) * 2)

    def swap(j):
        return pltpu.make_async_remote_copy(
            gb.at[2 * j + 1 - lane], pb.at[j], ps_s.at[j], ps_r.at[j],
            device_id=partner, device_id_type=MESH,
        )

    def chain(j, g):
        part = pl.ds(g * piece, piece)
        return pltpu.make_async_remote_copy(
            cs.at[j, part], cr.at[j, part], ch_s.at[j, g], ch_r.at[j, g],
            device_id=towards(j), device_id_type=MESH,
        )

    def spread(j, g):
        part = pl.ds(g * piece, piece)
        return pltpu.make_async_remote_copy(
            wn.at[mine(j), part], wn.at[mine(j), part], ag_s.at[j, g], ag_r.at[j, g],
            device_id=back(j), device_id_type=MESH,
        )

    def across(j, g, m):
        part = pl.ds(g * piece, piece)
        return pltpu.make_async_remote_copy(
            wn.at[m, part], wn.at[m, part], ap_s.at[j, g], ap_r.at[j, g],
            device_id=partner, device_id_type=MESH,
        )

    def wide(h):
        return pl.ds(pl.multiple_of((hd * heads + h) * size, size), size)

    def deal(b, h, p):
        peer = lax.rem(hd + p, nh)
        return pltpu.make_async_remote_copy(
            ob.at[b, h, pl.ds(pl.multiple_of(peer * share, share), share)],
            out.at[b, :, wide(h)],
            a_s.at[b, h, p - 1], a_r.at[b, h, p - 1],
            device_id=(peer, tok), device_id_type=MESH,
        )

    def arrive(b, h, p):
        source = lax.rem(hd + nh - p, nh)
        return pltpu.make_async_remote_copy(
            ob.at[b, h, pl.ds(pl.multiple_of(hd * share, share), share)],
            out.at[b, :, pl.ds(pl.multiple_of((source * heads + h) * size, size), size)],
            a_s.at[b, h, p - 1], a_r.at[b, h, p - 1],
            device_id=(source, tok), device_id_type=MESH,
        )

    def keep(b, h):
        return pltpu.make_async_copy(
            ob.at[b, h, pl.ds(pl.multiple_of(hd * share, share), share)],
            out.at[b, :, wide(h)], a_l.at[b, h],
        )

    def deal_all(b, h):
        for p in range(nh - 1, 0, -1):
            deal(b, h, p).start()
        keep(b, h).start()

    def wait_load(h, picks):
        for at in picks:
            load(at, h).wait()

    def gradients(h):
        wait_load(h, range(5))
        keys = kb[h]
        gate = wf[0, h].astype(BF)
        up = wf[1, h].astype(BF)
        down = wf[2, h].astype(BF)
        wh[0, h] = gate
        wh[1, h] = up
        wh[2, h] = down
        zg = mm(keys, gate)
        zu = mm(keys, up)
        sig = 1.0 / (1.0 + jnp.exp(-zg))
        silu = zg * sig
        hidden = (silu * zu).astype(BF)
        line = jnp.broadcast_to(rates[pl.ds(h, 1), :], (128, rows))
        column = jnp.transpose(line)
        column = jnp.concatenate([column] * (size // 128), axis=1)
        dout = (-(column * vb[h].astype(F32))).astype(BF)
        dh = mm_nt(dout, down)
        dzu = (dh * silu).astype(BF)
        dzg = (dh * zu * sig * (1.0 + zg * (1.0 - sig))).astype(BF)
        base = KINDS * h
        gb[base] = mm_tn(keys, dzg).astype(BF)
        gb[base + 1] = mm_tn(keys, dzu).astype(BF)
        gb[base + 2] = mm_tn(hidden, dout).astype(BF)
        for kind in range(KINDS):
            m = base + kind

            @pl.when(lax.rem(m, 2) != lane)
            def _():
                swap(m // 2).start()

    def first(h):
        wait_load(h, (5,))
        ob[0, h] = fast_apply(qb[0, h], wh[0, h], wh[1, h], wh[2, h])
        deal_all(0, h)

    def own(h, step):
        for kind in range(KINDS):
            m = KINDS * h + kind

            @pl.when(lax.rem(m, 2) == lane)
            def _():
                step(m // 2)

    def start_step(j):
        swap(j).wait_recv()

        @pl.when(is_start(j))
        def _():
            cs[j] = (gb[mine(j)].astype(F32) + pb[j].astype(F32)).astype(BF)
            for g in range(PIECES):
                chain(j, g).start()

    def pass_step(j):
        @pl.when(jnp.logical_not(is_start(j)) & jnp.logical_not(is_owner(j)))
        def _():
            for g in range(PIECES):
                part = pl.ds(g * piece, piece)
                chain(j, g).wait_recv()
                cs[j, part] = (
                    gb[mine(j), part].astype(F32)
                    + pb[j, part].astype(F32)
                    + cr[j, part].astype(F32)
                ).astype(BF)
                chain(j, g).start()

    @pl.loop(0, 2 * heads)
    def _(t):
        @pl.when(t < heads)
        def _():
            gradients(t)

        @pl.when(t >= heads)
        def _():
            first(t - heads)

        @pl.when((t >= 1) & (t <= heads))
        def _():
            own(t - 1, start_step)

        @pl.when((t >= LAG) & (t < heads + LAG))
        def _():
            own(t - LAG, pass_step)

    @pl.loop(0, pairs)
    def _(j):
        m = mine(j)

        @pl.when((m < count) & is_owner(j))
        def _():
            for g in range(PIECES):
                chain(j, g).wait_recv()
            grad = gb[m].astype(F32) + pb[j].astype(F32) + cr[j].astype(F32)
            scale = jnp.sqrt(jnp.sum(grad * grad)) + 1e-07
            x = grad / scale
            for _ in range(NS_STEPS):
                xb = x.astype(BF)
                gram = mm_tn(xb, xb)
                half = gram.astype(BF)
                poly = coef_second * gram + coef_third * mm(half, half)
                x = coef_first * x + mm(xb, poly.astype(BF))
            wn[m] = (wf[lax.rem(m, KINDS), m // KINDS] - x).astype(BF)
            for g in range(PIECES):
                spread(j, g).start()
                across(j, g, m).start()

    def second(h):
        for kind in range(KINDS):
            m = KINDS * h + kind

            @pl.when(lax.rem(m, 2) != lane)
            def _():
                for g in range(PIECES):
                    across(m // 2, g, m).wait_recv()

        @pl.when(h >= 0)
        def _():
            wait_load(h, (6,))
            base = KINDS * h
            ob[1, h] = fast_apply(qb[1, h], wn[base], wn[base + 1], wn[base + 2])
            deal_all(1, h)

    @pl.loop(0, pairs)
    def _(j):
        m = mine(j)

        @pl.when((m < count) & jnp.logical_not(is_owner(j)))
        def _():
            for g in range(PIECES):
                spread(j, g).wait_recv()

                @pl.when(jnp.logical_not(is_start(j)))
                def _():
                    spread(j, g).start()

                across(j, g, m).start()

        h = jnp.maximum(2 * j - 1, 0) // KINDS

        @pl.when((j >= 1) & (h < heads) & ((KINDS * h + KINDS - 1) // 2 == j))
        def _():
            second(h)

    @pl.loop(0, pairs)
    def _(j):
        m = mine(j)

        @pl.when(2 * j + 1 - lane < count)
        def _():
            swap(j).wait_send()

        @pl.when(m < count)
        def _():
            for g in range(PIECES):
                across(j, g, m).wait_send()

                @pl.when(jnp.logical_not(is_owner(j)))
                def _():
                    chain(j, g).wait_send()

                @pl.when(jnp.logical_not(is_start(j)))
                def _():
                    spread(j, g).wait_send()

    for b in range(2):
        @pl.loop(0, heads)
        def _(h):
            for p in range(1, nh):
                arrive(b, h, p).wait_recv()
                deal(b, h, p).wait_send()
            keep(b, h).wait()


def solution(mesh):
    nh = mesh.shape["head"]
    nz = mesh.shape["tok"] // 2

    def local(queries, key_rows, value_rows, step_rates, gate_fast, up_fast, down_fast):
        heads, size, _ = gate_fast.shape
        rows = key_rows.shape[0]
        pairs = (KINDS * heads + 1) // 2
        anywhere = pl.BlockSpec(memory_space=pl.ANY)
        dma = pltpu.SemaphoreType.DMA
        return pl.pallas_call(
            functools.partial(kernel, nh, nz),
            out_shape=jax.ShapeDtypeStruct((2, rows // nh, nh * heads * size), BF),
            in_specs=[
                anywhere, anywhere, anywhere,
                pl.BlockSpec(memory_space=pltpu.VMEM),
                anywhere, anywhere, anywhere,
            ],
            out_specs=anywhere,
            scratch_shapes=[
                pltpu.VMEM((2, heads, rows, size), BF),
                pltpu.VMEM((heads, rows, size), BF),
                pltpu.VMEM((heads, rows, size), BF),
                pltpu.VMEM((KINDS, heads, size, size), F32),
                pltpu.VMEM((KINDS, heads, size, size), BF),
                pltpu.VMEM((2 * pairs, size, size), BF),
                pltpu.VMEM((pairs, size, size), BF),
                pltpu.VMEM((pairs, size, size), BF),
                pltpu.VMEM((pairs, size, size), BF),
                pltpu.VMEM((2 * pairs, size, size), BF),
                pltpu.VMEM((2, heads, rows, size), BF),
                dma((7, heads)),
                dma((pairs,)), dma((pairs,)),
                dma((pairs, PIECES)), dma((pairs, PIECES)),
                dma((pairs, PIECES)), dma((pairs, PIECES)),
                dma((pairs, PIECES)), dma((pairs, PIECES)),
                dma((2, heads, nh - 1)), dma((2, heads, nh - 1)),
                dma((2, heads)),
            ],
            compiler_params=pltpu.CompilerParams(
                collective_id=0, has_side_effects=True, vmem_limit_bytes=48 << 20
            ),
        )(queries, key_rows, value_rows, step_rates, gate_fast, up_fast, down_fast)

    placed = (
        P(None, "tok", "head"),
        P("tok", "head"),
        P("tok", "head"),
        P("head", "tok"),
        P("head", None, None),
        P("head", None, None),
        P("head", None, None),
    )
    return jax.shard_map(
        local, mesh=mesh, in_specs=placed, out_specs=P(None, ("tok", "head"), None), check_vma=False
    )
```

```python
import functools

import jax
import jax.numpy as jnp
from jax import lax
from jax.experimental import pallas as pl
from jax.experimental.pallas import tpu as pltpu
from jax.sharding import PartitionSpec as P

NS_STEPS = 3
KINDS = 3
PIECES = 2
EXTRA = 2
DEPTH = 4

coef_first = 3.4445
coef_second = -4.775
coef_third = 2.0315

MESH = pl.DeviceIdType.MESH
BF = jnp.bfloat16
F32 = jnp.float32


def mm(a, b):
    return jnp.dot(a, b, preferred_element_type=F32)


def mm_tn(a, b):
    return lax.dot_general(a, b, (((0,), (0,)), ((), ())), preferred_element_type=F32)


def mm_nt(a, b):
    return lax.dot_general(a, b, (((1,), (1,)), ((), ())), preferred_element_type=F32)


def fast_apply(x, gate, up, down):
    pre = mm(x, gate)
    hidden = (pre / (1.0 + jnp.exp(-pre)) * mm(x, up)).astype(BF)
    return mm(hidden, down).astype(BF)


def kernel(
    nh, nz, q_in, k_in, v_in, rates, g_in, u_in, d_in, out,
    qb, kb, vb, wf, wh, gb, pb, cs, cr, wn, ob,
    in_sem, ps_s, ps_r, ch_s, ch_r, ag_s, ag_r, ap_s, ap_r, a_s, a_r, a_l,
):
    heads, rows, size = kb.shape
    count = KINDS * heads
    pairs = pb.shape[0]
    piece = size // PIECES
    share = rows // nh
    hd = lax.axis_index("head")
    tok = lax.axis_index("tok")
    lane = lax.rem(tok, 2)
    z = tok // 2
    partner = (hd, z * 2 + 1 - lane)

    def cut(h):
        return pl.ds(h * size if isinstance(h, int) else pl.multiple_of(h * size, size), size)

    def load(at, h):
        src, dst = (
            (k_in.at[:, cut(h)], kb.at[h]),
            (g_in.at[h], wf.at[0, h]),
            (u_in.at[h], wf.at[1, h]),
            (v_in.at[:, cut(h)], vb.at[h]),
            (d_in.at[h], wf.at[2, h]),
            (q_in.at[0, :, cut(h)], qb.at[0, h]),
            (q_in.at[1, :, cut(h)], qb.at[1, h]),
        )[at]
        return pltpu.make_async_copy(src, dst, in_sem.at[at, h])

    for h in range(heads):
        for at in range(5):
            load(at, h).start()
    for h in range(heads):
        for at in (5, 6):
            load(at, h).start()

    barrier = pltpu.get_barrier_semaphore()
    pl.semaphore_signal(barrier, inc=1, device_id=partner, device_id_type=MESH)
    for p in range(1, nh):
        pl.semaphore_signal(
            barrier, inc=1, device_id=(lax.rem(hd + p, nh), tok), device_id_type=MESH
        )

    @pl.when(z > 0)
    def _():
        pl.semaphore_signal(barrier, inc=1, device_id=(hd, tok - 2), device_id_type=MESH)

    @pl.when(z < nz - 1)
    def _():
        pl.semaphore_signal(barrier, inc=1, device_id=(hd, tok + 2), device_id_type=MESH)

    inner = (z > 0).astype(jnp.int32) + (z < nz - 1).astype(jnp.int32)
    pl.semaphore_wait(barrier, nh + inner)

    def mine(j):
        return 2 * j + lane

    def side(j):
        return lax.rem(j, 2)

    def is_start(j):
        return z == (1 - side(j)) * (nz - 1)

    def is_owner(j):
        return z == side(j) * (nz - 1)

    def towards(j):
        return (hd, tok + (2 * side(j) - 1) * 2)

    def back(j):
        return (hd, tok - (2 * side(j) - 1) * 2)

    def swap(j):
        return pltpu.make_async_remote_copy(
            gb.at[2 * j + 1 - lane], pb.at[j], ps_s.at[j], ps_r.at[j],
            device_id=partner, device_id_type=MESH,
        )

    def chain(j, g):
        part = pl.ds(g * piece, piece)
        return pltpu.make_async_remote_copy(
            cs.at[j, part], cr.at[j, part], ch_s.at[j, g], ch_r.at[j, g],
            device_id=towards(j), device_id_type=MESH,
        )

    def spread(j, g):
        part = pl.ds(g * piece, piece)
        return pltpu.make_async_remote_copy(
            wn.at[mine(j), part], wn.at[mine(j), part], ag_s.at[j, g], ag_r.at[j, g],
            device_id=back(j), device_id_type=MESH,
        )

    def across(j, g, m):
        part = pl.ds(g * piece, piece)
        return pltpu.make_async_remote_copy(
            wn.at[m, part], wn.at[m, part], ap_s.at[j, g], ap_r.at[j, g],
            device_id=partner, device_id_type=MESH,
        )

    def launch(make, j, g):
        before = j + 2 * ((g - DEPTH) // PIECES)

        @pl.when(before >= 0)
        def _():
            make(before, (g - DEPTH) % PIECES).wait_send()

        make(j, g).start()

    def land(make, j, g):
        @pl.when(mine(j + 2 * ((g + DEPTH) // PIECES)) >= count)
        def _():
            make(j, g).wait_send()

    def wide(h):
        return pl.ds(pl.multiple_of((hd * heads + h) * size, size), size)

    def deal(b, h, p):
        peer = lax.rem(hd + p, nh)
        return pltpu.make_async_remote_copy(
            ob.at[b, h, pl.ds(pl.multiple_of(peer * share, share), share)],
            out.at[b, :, wide(h)],
            a_s.at[b, h, p - 1], a_r.at[b, h, p - 1],
            device_id=(peer, tok), device_id_type=MESH,
        )

    def arrive(b, h, p):
        source = lax.rem(hd + nh - p, nh)
        return pltpu.make_async_remote_copy(
            ob.at[b, h, pl.ds(pl.multiple_of(hd * share, share), share)],
            out.at[b, :, pl.ds(pl.multiple_of((source * heads + h) * size, size), size)],
            a_s.at[b, h, p - 1], a_r.at[b, h, p - 1],
            device_id=(source, tok), device_id_type=MESH,
        )

    def keep(b, h):
        return pltpu.make_async_copy(
            ob.at[b, h, pl.ds(pl.multiple_of(hd * share, share), share)],
            out.at[b, :, wide(h)], a_l.at[b, h],
        )

    def deal_all(b, h):
        for p in range(nh - 1, 0, -1):
            deal(b, h, p).start()
        keep(b, h).start()

    def wait_load(h, picks):
        for at in picks:
            load(at, h).wait()

    def gradients(h):
        wait_load(h, range(5))
        keys = kb[h]
        gate = wf[0, h].astype(BF)
        up = wf[1, h].astype(BF)
        down = wf[2, h].astype(BF)
        wh[0, h] = gate
        wh[1, h] = up
        wh[2, h] = down
        zg = mm(keys, gate)
        zu = mm(keys, up)
        sig = 1.0 / (1.0 + jnp.exp(-zg))
        silu = zg * sig
        hidden = (silu * zu).astype(BF)
        line = jnp.broadcast_to(rates[pl.ds(h, 1), :], (128, rows))
        column = jnp.transpose(line)
        column = jnp.concatenate([column] * (size // 128), axis=1)
        dout = (-(column * vb[h].astype(F32))).astype(BF)
        dh = mm_nt(dout, down)
        dzu = (dh * silu).astype(BF)
        dzg = (dh * zu * sig * (1.0 + zg * (1.0 - sig))).astype(BF)
        base = KINDS * h
        gb[base] = mm_tn(keys, dzg).astype(BF)
        gb[base + 1] = mm_tn(keys, dzu).astype(BF)
        gb[base + 2] = mm_tn(hidden, dout).astype(BF)
        for kind in range(KINDS):
            m = base + kind

            @pl.when(lax.rem(m, 2) != lane)
            def _():
                swap(m // 2).start()

    def first(h):
        wait_load(h, (5,))
        ob[0, h] = fast_apply(qb[0, h], wh[0, h], wh[1, h], wh[2, h])
        deal_all(0, h)

    def own(h, step):
        for kind in range(KINDS):
            m = KINDS * h + kind

            @pl.when(lax.rem(m, 2) == lane)
            def _():
                step(m // 2)

    def start_step(j):
        swap(j).wait_recv()

        @pl.when(is_start(j))
        def _():
            cs[j] = (gb[mine(j)].astype(F32) + pb[j].astype(F32)).astype(BF)
            for g in range(PIECES):
                launch(chain, j, g)

    def pass_step(j):
        @pl.when(jnp.logical_not(is_start(j)) & jnp.logical_not(is_owner(j)))
        def _():
            for g in range(PIECES):
                part = pl.ds(g * piece, piece)
                chain(j, g).wait_recv()
                cs[j, part] = (
                    gb[mine(j), part].astype(F32)
                    + pb[j, part].astype(F32)
                    + cr[j, part].astype(F32)
                ).astype(BF)
                launch(chain, j, g)

    lag = EXTRA + max(
        min((2 * j + 1) // KINDS, heads - 1) + 1 - (j // 2 + 1) for j in range(pairs)
    )
    turns = (pairs - 1) // 2 + nz - 1
    total = max(2 * heads, turns + lag)

    def reach(j):
        return jnp.where(side(j) == 0, nz - 1 - z, z)

    @pl.loop(0, total)
    def _(t):
        @pl.when(t < heads)
        def _():
            gradients(t)

        @pl.when((t >= heads) & (t < 2 * heads))
        def _():
            first(t - heads)

        @pl.when((t >= 1) & (t <= heads))
        def _():
            own(t - 1, start_step)

        for s in range(2):
            i = t - lag - reach(s)
            j = 2 * i + s

            @pl.when((i >= 0) & (j < pairs) & (mine(j) < count))
            def _():
                pass_step(j)

    @pl.loop(0, pairs)
    def _(j):
        m = mine(j)

        @pl.when((m < count) & is_owner(j))
        def _():
            for g in range(PIECES):
                chain(j, g).wait_recv()
            grad = gb[m].astype(F32) + pb[j].astype(F32) + cr[j].astype(F32)
            scale = jnp.sqrt(jnp.sum(grad * grad)) + 1e-07
            x = grad / scale
            for _ in range(NS_STEPS):
                xb = x.astype(BF)
                gram = mm_tn(xb, xb)
                half = gram.astype(BF)
                poly = coef_second * gram + coef_third * mm(half, half)
                x = coef_first * x + mm(xb, poly.astype(BF))
            wn[m] = (wf[lax.rem(m, KINDS), m // KINDS] - x).astype(BF)
            for g in range(PIECES):
                launch(spread, j, g)
                across(j, g, m).start()

    def second(h):
        for kind in range(KINDS):
            m = KINDS * h + kind

            @pl.when(lax.rem(m, 2) != lane)
            def _():
                for g in range(PIECES):
                    across(m // 2, g, m).wait_recv()

        wait_load(h, (6,))
        base = KINDS * h
        ob[1, h] = fast_apply(qb[1, h], wn[base], wn[base + 1], wn[base + 2])
        deal_all(1, h)

    def relay(j):
        m = mine(j)
        for g in range(PIECES):
            spread(j, g).wait_recv()

            @pl.when(jnp.logical_not(is_start(j)))
            def _():
                launch(spread, j, g)

            across(j, g, m).start()

    def away(j):
        return jnp.where(side(j) == 0, z, nz - 1 - z)

    @pl.loop(0, (pairs - 1) // 2 + nz)
    def _(t):
        for s in range(2):
            i = t - away(s)
            j = 2 * i + s

            @pl.when((i >= 0) & (j < pairs) & (mine(j) < count) & jnp.logical_not(is_owner(j)))
            def _():
                relay(j)

        @pl.loop(0, heads)
        def _(h):
            top = (KINDS * h + KINDS - 1) // 2
            below = top - 1
            due = jnp.maximum(top // 2 + away(top), below // 2 + away(below))

            @pl.when(due == t)
            def _():
                second(h)

    @pl.loop(0, pairs)
    def _(j):
        m = mine(j)

        @pl.when(2 * j + 1 - lane < count)
        def _():
            swap(j).wait_send()

        @pl.when(m < count)
        def _():
            for g in range(PIECES):
                across(j, g, m).wait_send()

                @pl.when(jnp.logical_not(is_owner(j)))
                def _():
                    land(chain, j, g)

                @pl.when(jnp.logical_not(is_start(j)))
                def _():
                    land(spread, j, g)

    for b in range(2):
        @pl.loop(0, heads)
        def _(h):
            for p in range(1, nh):
                arrive(b, h, p).wait_recv()
                deal(b, h, p).wait_send()
            keep(b, h).wait()


def solution(mesh):
    nh = mesh.shape["head"]
    nz = mesh.shape["tok"] // 2

    def local(queries, key_rows, value_rows, step_rates, gate_fast, up_fast, down_fast):
        heads, size, _ = gate_fast.shape
        rows = key_rows.shape[0]
        pairs = (KINDS * heads + 1) // 2
        anywhere = pl.BlockSpec(memory_space=pl.ANY)
        dma = pltpu.SemaphoreType.DMA
        return pl.pallas_call(
            functools.partial(kernel, nh, nz),
            out_shape=jax.ShapeDtypeStruct((2, rows // nh, nh * heads * size), BF),
            in_specs=[
                anywhere, anywhere, anywhere,
                pl.BlockSpec(memory_space=pltpu.VMEM),
                anywhere, anywhere, anywhere,
            ],
            out_specs=anywhere,
            scratch_shapes=[
                pltpu.VMEM((2, heads, rows, size), BF),
                pltpu.VMEM((heads, rows, size), BF),
                pltpu.VMEM((heads, rows, size), BF),
                pltpu.VMEM((KINDS, heads, size, size), F32),
                pltpu.VMEM((KINDS, heads, size, size), BF),
                pltpu.VMEM((2 * pairs, size, size), BF),
                pltpu.VMEM((pairs, size, size), BF),
                pltpu.VMEM((pairs, size, size), BF),
                pltpu.VMEM((pairs, size, size), BF),
                pltpu.VMEM((2 * pairs, size, size), BF),
                pltpu.VMEM((2, heads, rows, size), BF),
                dma((7, heads)),
                dma((pairs,)), dma((pairs,)),
                dma((pairs, PIECES)), dma((pairs, PIECES)),
                dma((pairs, PIECES)), dma((pairs, PIECES)),
                dma((pairs, PIECES)), dma((pairs, PIECES)),
                dma((2, heads, nh - 1)), dma((2, heads, nh - 1)),
                dma((2, heads)),
            ],
            compiler_params=pltpu.CompilerParams(
                collective_id=0, has_side_effects=True, vmem_limit_bytes=67043328
            ),
        )(queries, key_rows, value_rows, step_rates, gate_fast, up_fast, down_fast)

    placed = (
        P(None, "tok", "head"),
        P("tok", "head"),
        P("tok", "head"),
        P("head", "tok"),
        P("head", None, None),
        P("head", None, None),
        P("head", None, None),
    )
    return jax.shard_map(
        local, mesh=mesh, in_specs=placed, out_specs=P(None, ("tok", "head"), None), check_vma=False
    )
```

```python
import functools

import jax
import jax.numpy as jnp
from jax import lax
from jax.experimental import pallas as pl
from jax.experimental.pallas import tpu as pltpu
from jax.sharding import PartitionSpec as P

NS_STEPS = 3
KINDS = 3
PIECES = 4
EXTRA = 3
DEPTH = 16

coef_first = 3.4445
coef_second = -4.775
coef_third = 2.0315

MESH = pl.DeviceIdType.MESH
BF = jnp.bfloat16
F32 = jnp.float32


def mm(a, b):
    return jnp.dot(a, b, preferred_element_type=F32)


def mm_tn(a, b):
    return lax.dot_general(a, b, (((0,), (0,)), ((), ())), preferred_element_type=F32)


def mm_nt(a, b):
    return lax.dot_general(a, b, (((1,), (1,)), ((), ())), preferred_element_type=F32)


def fast_apply(x, gate, up, down):
    pre = mm(x, gate)
    hidden = (pre / (1.0 + jnp.exp(-pre)) * mm(x, up)).astype(BF)
    return mm(hidden, down).astype(BF)


def kernel(
    nh, nz, q_in, k_in, v_in, rates, g_in, u_in, d_in, out,
    qb, kb, vb, wf, wh, gb, pb, cs, cr, wn, ob,
    in_sem, ps_s, ps_r, ch_s, ch_r, ag_s, ag_r, ap_s, ap_r, a_s, a_r, a_l,
):
    heads, rows, size = kb.shape
    count = KINDS * heads
    pairs = pb.shape[0]
    piece = size // PIECES
    share = rows // nh
    hd = lax.axis_index("head")
    tok = lax.axis_index("tok")
    lane = lax.rem(tok, 2)
    z = tok // 2
    partner = (hd, z * 2 + 1 - lane)

    def cut(h):
        return pl.ds(h * size if isinstance(h, int) else pl.multiple_of(h * size, size), size)

    def load(at, h):
        src, dst = (
            (k_in.at[:, cut(h)], kb.at[h]),
            (g_in.at[h], wf.at[0, h]),
            (u_in.at[h], wf.at[1, h]),
            (v_in.at[:, cut(h)], vb.at[h]),
            (d_in.at[h], wf.at[2, h]),
            (q_in.at[0, :, cut(h)], qb.at[0, h]),
            (q_in.at[1, :, cut(h)], qb.at[1, h]),
        )[at]
        return pltpu.make_async_copy(src, dst, in_sem.at[at, h])

    for h in range(heads):
        for at in range(5):
            load(at, h).start()
    for h in range(heads):
        for at in (5, 6):
            load(at, h).start()

    barrier = pltpu.get_barrier_semaphore()
    pl.semaphore_signal(barrier, inc=1, device_id=partner, device_id_type=MESH)
    for p in range(1, nh):
        pl.semaphore_signal(
            barrier, inc=1, device_id=(lax.rem(hd + p, nh), tok), device_id_type=MESH
        )

    @pl.when(z > 0)
    def _():
        pl.semaphore_signal(barrier, inc=1, device_id=(hd, tok - 2), device_id_type=MESH)

    @pl.when(z < nz - 1)
    def _():
        pl.semaphore_signal(barrier, inc=1, device_id=(hd, tok + 2), device_id_type=MESH)

    inner = (z > 0).astype(jnp.int32) + (z < nz - 1).astype(jnp.int32)
    pl.semaphore_wait(barrier, nh + inner)

    def mine(j):
        return 2 * j + lane

    def side(j):
        return lax.rem(j, 2)

    def is_start(j):
        return z == (1 - side(j)) * (nz - 1)

    def is_owner(j):
        return z == side(j) * (nz - 1)

    def towards(j):
        return (hd, tok + (2 * side(j) - 1) * 2)

    def back(j):
        return (hd, tok - (2 * side(j) - 1) * 2)

    def swap(j):
        return pltpu.make_async_remote_copy(
            gb.at[2 * j + 1 - lane], pb.at[j], ps_s.at[j], ps_r.at[j],
            device_id=partner, device_id_type=MESH,
        )

    def chain(j, g):
        part = pl.ds(g * piece, piece)
        return pltpu.make_async_remote_copy(
            cs.at[j, part], cr.at[j, part], ch_s.at[j, g], ch_r.at[j, g],
            device_id=towards(j), device_id_type=MESH,
        )

    def spread(j, g):
        part = pl.ds(g * piece, piece)
        return pltpu.make_async_remote_copy(
            wn.at[mine(j), part], wn.at[mine(j), part], ag_s.at[j, g], ag_r.at[j, g],
            device_id=back(j), device_id_type=MESH,
        )

    def across(j, g, m):
        part = pl.ds(g * piece, piece)
        return pltpu.make_async_remote_copy(
            wn.at[m, part], wn.at[m, part], ap_s.at[j, g], ap_r.at[j, g],
            device_id=partner, device_id_type=MESH,
        )

    def launch(make, j, g):
        before = j + 2 * ((g - DEPTH) // PIECES)

        @pl.when(before >= 0)
        def _():
            make(before, (g - DEPTH) % PIECES).wait_send()

        make(j, g).start()

    def land(make, j, g):
        @pl.when(mine(j + 2 * ((g + DEPTH) // PIECES)) >= count)
        def _():
            make(j, g).wait_send()

    def wide(h):
        return pl.ds(pl.multiple_of((hd * heads + h) * size, size), size)

    def deal(b, h, p):
        peer = lax.rem(hd + p, nh)
        return pltpu.make_async_remote_copy(
            ob.at[b, h, pl.ds(pl.multiple_of(peer * share, share), share)],
            out.at[b, :, wide(h)],
            a_s.at[b, h, p - 1], a_r.at[b, h, p - 1],
            device_id=(peer, tok), device_id_type=MESH,
        )

    def arrive(b, h, p):
        source = lax.rem(hd + nh - p, nh)
        return pltpu.make_async_remote_copy(
            ob.at[b, h, pl.ds(pl.multiple_of(hd * share, share), share)],
            out.at[b, :, pl.ds(pl.multiple_of((source * heads + h) * size, size), size)],
            a_s.at[b, h, p - 1], a_r.at[b, h, p - 1],
            device_id=(source, tok), device_id_type=MESH,
        )

    def keep(b, h):
        return pltpu.make_async_copy(
            ob.at[b, h, pl.ds(pl.multiple_of(hd * share, share), share)],
            out.at[b, :, wide(h)], a_l.at[b, h],
        )

    def deal_all(b, h):
        for p in range(nh - 1, 0, -1):
            deal(b, h, p).start()
        keep(b, h).start()

    def wait_load(h, picks):
        for at in picks:
            load(at, h).wait()

    def gradients(h):
        wait_load(h, range(5))
        keys = kb[h]
        gate = wf[0, h].astype(BF)
        up = wf[1, h].astype(BF)
        down = wf[2, h].astype(BF)
        wh[0, h] = gate
        wh[1, h] = up
        wh[2, h] = down
        zg = mm(keys, gate)
        zu = mm(keys, up)
        sig = 1.0 / (1.0 + jnp.exp(-zg))
        silu = zg * sig
        hidden = (silu * zu).astype(BF)
        line = jnp.broadcast_to(rates[pl.ds(h, 1), :], (128, rows))
        column = jnp.transpose(line)
        column = jnp.concatenate([column] * (size // 128), axis=1)
        dout = (-(column * vb[h].astype(F32))).astype(BF)
        dh = mm_nt(dout, down)
        dzu = (dh * silu).astype(BF)
        dzg = (dh * zu * sig * (1.0 + zg * (1.0 - sig))).astype(BF)
        base = KINDS * h
        gb[base] = mm_tn(keys, dzg).astype(BF)
        gb[base + 1] = mm_tn(keys, dzu).astype(BF)
        gb[base + 2] = mm_tn(hidden, dout).astype(BF)
        for kind in range(KINDS):
            m = base + kind

            @pl.when(lax.rem(m, 2) != lane)
            def _():
                swap(m // 2).start()

    def first(h):
        wait_load(h, (5,))
        ob[0, h] = fast_apply(qb[0, h], wh[0, h], wh[1, h], wh[2, h])
        deal_all(0, h)

    def own(h, step):
        for kind in range(KINDS):
            m = KINDS * h + kind

            @pl.when(lax.rem(m, 2) == lane)
            def _():
                step(m // 2)

    def start_step(j):
        swap(j).wait_recv()

        @pl.when(is_start(j))
        def _():
            cs[j] = (gb[mine(j)].astype(F32) + pb[j].astype(F32)).astype(BF)
            for g in range(PIECES):
                launch(chain, j, g)

    def pass_step(j):
        @pl.when(jnp.logical_not(is_start(j)) & jnp.logical_not(is_owner(j)))
        def _():
            for g in range(PIECES):
                part = pl.ds(g * piece, piece)
                chain(j, g).wait_recv()
                cs[j, part] = (
                    gb[mine(j), part].astype(F32)
                    + pb[j, part].astype(F32)
                    + cr[j, part].astype(F32)
                ).astype(BF)
                launch(chain, j, g)

    lag = EXTRA + max(
        min((2 * j + 1) // KINDS, heads - 1) + 1 - (j // 2 + 1) for j in range(pairs)
    )
    turns = (pairs - 1) // 2 + nz - 1
    total = max(2 * heads, turns + lag)

    def reach(j):
        return jnp.where(side(j) == 0, nz - 1 - z, z)

    @pl.loop(0, total)
    def _(t):
        @pl.when(t < heads)
        def _():
            gradients(t)

        @pl.when((t >= heads) & (t < 2 * heads))
        def _():
            first(t - heads)

        @pl.when((t >= 1) & (t <= heads))
        def _():
            own(t - 1, start_step)

        for s in range(2):
            i = t - lag - reach(s)
            j = 2 * i + s

            @pl.when((i >= 0) & (j < pairs) & (mine(j) < count))
            def _():
                pass_step(j)

    @pl.loop(0, pairs)
    def _(j):
        m = mine(j)

        @pl.when((m < count) & is_owner(j))
        def _():
            for g in range(PIECES):
                chain(j, g).wait_recv()
            grad = gb[m].astype(F32) + pb[j].astype(F32) + cr[j].astype(F32)
            scale = jnp.sqrt(jnp.sum(grad * grad)) + 1e-07
            x = grad / scale
            for _ in range(NS_STEPS):
                xb = x.astype(BF)
                gram = mm_tn(xb, xb)
                half = gram.astype(BF)
                poly = coef_second * gram + coef_third * mm(half, half)
                x = coef_first * x + mm(xb, poly.astype(BF))
            wn[m] = (wf[lax.rem(m, KINDS), m // KINDS] - x).astype(BF)
            for g in range(PIECES):
                launch(spread, j, g)
                across(j, g, m).start()

    def second(h):
        for kind in range(KINDS):
            m = KINDS * h + kind

            @pl.when(lax.rem(m, 2) != lane)
            def _():
                for g in range(PIECES):
                    across(m // 2, g, m).wait_recv()

        wait_load(h, (6,))
        base = KINDS * h
        ob[1, h] = fast_apply(qb[1, h], wn[base], wn[base + 1], wn[base + 2])
        deal_all(1, h)

    def relay(j):
        m = mine(j)
        for g in range(PIECES):
            spread(j, g).wait_recv()

            @pl.when(jnp.logical_not(is_start(j)))
            def _():
                launch(spread, j, g)

            across(j, g, m).start()

    def away(j):
        return jnp.where(side(j) == 0, z, nz - 1 - z)

    @pl.loop(0, (pairs - 1) // 2 + nz)
    def _(t):
        for s in range(2):
            i = t - away(s)
            j = 2 * i + s

            @pl.when((i >= 0) & (j < pairs) & (mine(j) < count) & jnp.logical_not(is_owner(j)))
            def _():
                relay(j)

        @pl.loop(0, heads)
        def _(h):
            top = (KINDS * h + KINDS - 1) // 2
            below = top - 1
            due = jnp.maximum(top // 2 + away(top), below // 2 + away(below))

            @pl.when(due == t)
            def _():
                second(h)

    @pl.loop(0, pairs)
    def _(j):
        m = mine(j)

        @pl.when(2 * j + 1 - lane < count)
        def _():
            swap(j).wait_send()

        @pl.when(m < count)
        def _():
            for g in range(PIECES):
                across(j, g, m).wait_send()

                @pl.when(jnp.logical_not(is_owner(j)))
                def _():
                    land(chain, j, g)

                @pl.when(jnp.logical_not(is_start(j)))
                def _():
                    land(spread, j, g)

    for b in range(2):
        @pl.loop(0, heads)
        def _(h):
            for p in range(1, nh):
                arrive(b, h, p).wait_recv()
                deal(b, h, p).wait_send()
            keep(b, h).wait()


def solution(mesh):
    nh = mesh.shape["head"]
    nz = mesh.shape["tok"] // 2

    def local(queries, key_rows, value_rows, step_rates, gate_fast, up_fast, down_fast):
        heads, size, _ = gate_fast.shape
        rows = key_rows.shape[0]
        pairs = (KINDS * heads + 1) // 2
        anywhere = pl.BlockSpec(memory_space=pl.ANY)
        dma = pltpu.SemaphoreType.DMA
        return pl.pallas_call(
            functools.partial(kernel, nh, nz),
            out_shape=jax.ShapeDtypeStruct((2, rows // nh, nh * heads * size), BF),
            in_specs=[
                anywhere, anywhere, anywhere,
                pl.BlockSpec(memory_space=pltpu.VMEM),
                anywhere, anywhere, anywhere,
            ],
            out_specs=anywhere,
            scratch_shapes=[
                pltpu.VMEM((2, heads, rows, size), BF),
                pltpu.VMEM((heads, rows, size), BF),
                pltpu.VMEM((heads, rows, size), BF),
                pltpu.VMEM((KINDS, heads, size, size), F32),
                pltpu.VMEM((KINDS, heads, size, size), BF),
                pltpu.VMEM((2 * pairs, size, size), BF),
                pltpu.VMEM((pairs, size, size), BF),
                pltpu.VMEM((pairs, size, size), BF),
                pltpu.VMEM((pairs, size, size), BF),
                pltpu.VMEM((2 * pairs, size, size), BF),
                pltpu.VMEM((2, heads, rows, size), BF),
                dma((7, heads)),
                dma((pairs,)), dma((pairs,)),
                dma((pairs, PIECES)), dma((pairs, PIECES)),
                dma((pairs, PIECES)), dma((pairs, PIECES)),
                dma((pairs, PIECES)), dma((pairs, PIECES)),
                dma((2, heads, nh - 1)), dma((2, heads, nh - 1)),
                dma((2, heads)),
            ],
            compiler_params=pltpu.CompilerParams(
                collective_id=0, has_side_effects=True, vmem_limit_bytes=67043328
            ),
        )(queries, key_rows, value_rows, step_rates, gate_fast, up_fast, down_fast)

    placed = (
        P(None, "tok", "head"),
        P("tok", "head"),
        P("tok", "head"),
        P("head", "tok"),
        P("head", None, None),
        P("head", None, None),
        P("head", None, None),
    )
    return jax.shard_map(
        local, mesh=mesh, in_specs=placed, out_specs=P(None, ("tok", "head"), None), check_vma=False
    )
```
